512 devices in a mesh: row: 32 (over z, y_lo), col: 8 (over x, core), rep: 2 (over y_hi).
Axes of the slice: x: 4, y: 4 (y_hi: 2, y_lo: 2; y = y_hi * 2 + y_lo), z: 16, core: 2. Of those that a mesh axis runs over, the one named last changes fastest.
Arguments:
- left_values: float32 [32, 2, 8, 2, 8, 2, 128, 128], P('row', 'rep', 'col'), may hold values from -0.5 to 0.5
- left_rows: int32 [32, 2, 8, 2, 8, 2], P('row', 'rep', 'col'), may hold values from 0 to 3, as said below
- right_values: float32 [2, 32, 8, 8, 4, 128, 128], P('rep', 'row', 'col'), may hold values from -1.5 to 1.5
- right_cols: int32 [2, 32, 8, 8, 4], P('rep', 'row', 'col'), may hold values from 0 to 7
- result_slots: int32 [32, 8, 24], P('row', 'col'), may hold values from 0 to 31, as said below
Outputs:
- result_blocks: float32 [32, 8, 24, 128, 128], P('row', 'col', 'rep')
The draws below stay inside these ranges and needn't reach their ends.
Inputs may be any that keep to these rules, and one draw needn't show every extreme that they name: `result_slots`: within one result tile the 24 slots are distinct; slot value p stands for the block at block row p // 8 and block column p % 8 of the tile. `left_rows`: the 2 block rows of one block column of a panel are distinct.
All inputs are finite; a program needn't handle non-finite values.
Results may differ from the reference program's by a relative error of at most 0.0003.
Values sent between devices are 32-bit elements; how exact they have to be, the bound alone decides.
A program may use at most 64 MiB of HBM per device.

```python
import jax
import jax.numpy as jnp
from jax import lax

ROW_TILES = 32
COL_TILES = 8
LAYERS = 2
BS = 128
KB = 8
BPR = 4
LPB = 2
STEPS = 4
RB = 4
CB = 8
NC = 24
M_SLOTS = 2


def draw_result_slots(key, part):
    tile_keys = jax.random.split(key, ROW_TILES * COL_TILES)

    def pick_slots(tile_key):
        return jax.random.permutation(tile_key, RB * CB)[:NC].astype(jnp.int32)
    return jax.vmap(pick_slots)(tile_keys).reshape(ROW_TILES, COL_TILES, NC)


def draw_left_rows(key, part):
    count = ROW_TILES * LAYERS * COL_TILES * M_SLOTS * KB
    column_keys = jax.random.split(jax.random.fold_in(key, 7), count)

    def pick_rows(column_key):
        return jax.random.permutation(column_key, RB)[:LPB].astype(jnp.int32)
    return jax.vmap(pick_rows)(column_keys).reshape(ROW_TILES, LAYERS, COL_TILES, M_SLOTS, KB, LPB)


def set_ends(array, key, low, largest):
    shape = array.shape
    spot = [jax.random.randint(jax.random.fold_in(key, axis), (), 0, shape[axis]) for axis in range(len(shape))]
    array = array.at[tuple(spot)].set(low)
    longest = shape.index(max(shape))
    spot[longest] = (spot[longest] + 1) % shape[longest]
    return array.at[tuple(spot)].set(largest)


def steps_of(stream_key, extent, shards, smallest, largest):
    def one(dim, shards_of):
        draws = jax.random.uniform(jax.random.fold_in(jax.random.fold_in(stream_key, 6), dim), (shards_of,), jnp.float32, smallest / len(shards), largest / len(shards))
        return jnp.repeat(jnp.exp(draws), extent[dim] // shards_of).reshape((-1,) + (1,) * (len(extent) - dim - 1))

    gain = one(*shards[0])
    for cut in shards[1:]:
        gain = gain * one(*cut)
    return gain


def gaussian(key, dims, scale, bound, cuts=(), held_as=jnp.bfloat16):
    factor_of = steps_of(key, dims, cuts, -0.22, 0.18) if cuts else 1.0
    drawn = jax.random.normal(key, dims, jnp.float32) * scale * factor_of
    return jnp.minimum(jnp.maximum(drawn, -bound), bound).astype(held_as)


def setup_inputs(seed: int = 0) -> dict:
    keys = jax.random.split(jax.random.key(seed), 6)
    left_values = gaussian(keys[0], (ROW_TILES, LAYERS, COL_TILES, M_SLOTS, KB, LPB, BS, BS), BS ** -0.5, 0.5, ((0, 32), (1, 2), (2, 8)), jnp.float32)
    left_rows = draw_left_rows(jax.random.fold_in(keys[5], 71), 0)
    right_values = gaussian(keys[2], (LAYERS, ROW_TILES, COL_TILES, KB, BPR, BS, BS), (2 * STEPS * KB * LPB * BPR // (RB * CB)) ** -0.5, 1.5, ((0, 2), (1, 32), (2, 8)), jnp.float32)
    right_cols = set_ends(jax.random.randint(keys[3], (LAYERS, ROW_TILES, COL_TILES, KB, BPR), 0, CB), jax.random.fold_in(keys[3], 1), 0, CB - 1).astype(jnp.int32)
    result_slots = draw_result_slots(jax.random.fold_in(keys[5], 71), 0)
    return {"left_values": left_values, "left_rows": left_rows, "right_values": right_values, "right_cols": right_cols, "result_slots": result_slots}


highest = lax.Precision.HIGHEST


def turn_products(left_blocks, left_places, right_blocks, right_places, listed):
    products = jnp.einsum("kaxy,kbyz->kabxz", left_blocks, right_blocks, precision=highest)
    block_codes = left_places[:, :, None] * CB + right_places[:, None, :]
    onehot = (block_codes[:, :, :, None] == listed[None, None, None, :]).astype(jnp.float32)
    return jnp.einsum("kabc,kabxz->cxz", onehot, products, precision=highest)


def reference(left_values, left_rows, right_values, right_cols, result_slots):
    layer_ids = jnp.arange(LAYERS, dtype=jnp.int32)
    column_ids = jnp.arange(COL_TILES, dtype=jnp.int32)

    def one_tile(tile_row, layer_index, tile_col):
        totals = jnp.zeros((NC, BS, BS), jnp.float32)
        for turn_index in range(STEPS):
            source = (tile_col + turn_index) % COL_TILES
            slot_index = (tile_col + turn_index) // COL_TILES
            right_row = (tile_row + turn_index) % ROW_TILES
            totals = totals + turn_products(
                left_values[tile_row, layer_index, source, slot_index],
                left_rows[tile_row, layer_index, source, slot_index],
                right_values[layer_index, right_row, tile_col],
                right_cols[layer_index, right_row, tile_col],
                result_slots[tile_row, tile_col])
        return totals

    def one_row(tile_row):
        def per_layer(layer_index):
            def per_column(tile_col):
                return one_tile(tile_row, layer_index, tile_col)
            return jax.vmap(per_column)(column_ids)
        layered = jax.vmap(per_layer)(layer_ids)
        return jnp.sum(layered, axis=0)

    return lax.map(one_row, jnp.arange(ROW_TILES, dtype=jnp.int32))
```

```python
import functools

import jax
import jax.numpy as jnp
from jax import lax
from jax.experimental import pallas as pl
from jax.experimental.pallas import tpu as pltpu
from jax.sharding import PartitionSpec as P

BS = 128
KB = 8
BPR = 4
LPB = 2
RB = 4
CB = 8
NC = 24
STRIPS = 4
LANES = BS // STRIPS
HALF = KB // 2
OWNED = NC // 2
PACKS = OWNED // STRIPS
UNIT = HALF * BS + 8
PANEL = HALF * LPB * BS + 8
STAGES = 3 * STRIPS
MESH = pl.DeviceIdType.MESH
f32 = jnp.float32
bf16 = jnp.bfloat16


def lane_group():
    return lax.broadcasted_iota(jnp.int32, (BS, BS), 1) // LANES


def regroup(group, parts):
    picked = parts[STRIPS - 1]
    for b in range(STRIPS - 2, -1, -1):
        picked = jnp.where(group == b, parts[b], picked)
    return picked


def shifted(x, groups):
    by = (groups * LANES) % BS
    return x if by == 0 else pltpu.roll(x, by, 1)


def kernel(
    rows, columns,
    left_hbm, right_hbm, left_rows, right_cols, slots, out,
    raw, units, panels, left_hi, left_lo, right_hi, right_lo, sums,
    own, stage, relay, arrived,
    load_sem, left_load_sem, z_send, z_recv, y_send, y_recv, x_send, x_recv,
    hop_send, hop_recv, last_send, last_recv,
):
    row = lax.axis_index("row")
    col = lax.axis_index("col")
    rep = lax.axis_index("rep")
    odd = lax.rem(row, 2)
    core = lax.rem(col, 2)
    chip = lax.div(col, 2)
    chips = columns // 2
    even_row = odd == 0
    even_core = core == 0
    mate_row = row + 1 - 2 * odd
    up = (lax.rem(row + 2, rows), col, rep)
    down = (lax.rem(row + rows - 2, rows), col, rep)
    inner = (mate_row, col, rep)
    outer = (mate_row, col, 1 - rep)
    sibling = (row, col + 1 - 2 * core, rep)
    right = (row, lax.rem(col + 2, columns), rep)
    left = (row, lax.rem(col + columns - 2, columns), rep)
    far = (row, lax.rem(col - core + 4, columns) + 1 - core, rep)

    barrier = pltpu.get_barrier_semaphore()
    peers = (up, down, inner, outer, sibling, right, left, far)
    for peer in peers:
        pl.semaphore_signal(barrier, inc=1, device_id=peer, device_id_type=MESH)

    def load_right(half):
        part = pl.ds(half * HALF * BPR, HALF * BPR)
        return pltpu.make_async_copy(right_hbm.at[part], raw.at[part], load_sem.at[half])

    def load_left(slot, half):
        return pltpu.make_async_copy(
            left_hbm.at[slot, half],
            panels.at[4 * slot, half, pl.ds(0, HALF * LPB * BS)],
            left_load_sem.at[slot, half],
        )

    for half in range(2):
        load_right(half).start()
    for slot in range(2):
        for half in range(2):
            load_left(slot, half).start()

    group = lane_group()
    sub8 = lax.broadcasted_iota(jnp.int32, (8, BS), 0)
    group8 = lax.broadcasted_iota(jnp.int32, (8, BS), 1) // LANES

    for half in range(2):
        marks = jnp.zeros((8, BS), f32)
        for kk in range(HALF):
            for b in range(BPR):
                place = right_cols[(half * HALF + kk) * BPR + b].astype(f32)
                marks = jnp.where((sub8 == kk) & (group8 == b), place, marks)
        for h in range(STRIPS):
            units[h, half, pl.ds(HALF * BS, 8), :] = marks
    for slot in range(2):
        for half in range(2):
            marks = jnp.zeros((8, BS), f32)
            for e in range(HALF * LPB):
                place = left_rows[(slot * KB + half * HALF) * LPB + e].astype(f32)
                marks = jnp.where(sub8 == e, place, marks)
            panels[4 * slot, half, pl.ds(HALF * LPB * BS, 8), :] = marks

    def pack(h, half):
        def one(kk, carry):
            k = half * HALF + kk
            parts = [shifted(raw[k * BPR + b], b - h) for b in range(BPR)]
            units[h, half, pl.ds(pl.multiple_of(kk * BS, BS), BS), :] = regroup(group, parts)
            return carry

        lax.fori_loop(0, HALF, one, 0)

    def z_copy(g, source, target):
        h = lax.div(g, 3)
        return pltpu.make_async_remote_copy(
            src_ref=units.at[h, source], dst_ref=units.at[h, target],
            send_sem=z_send.at[g], recv_sem=z_recv.at[g], device_id=down, device_id_type=MESH,
        )

    def y_copy(g, source, target):
        h = lax.div(g, 3)
        return pltpu.make_async_remote_copy(
            src_ref=units.at[h, source], dst_ref=units.at[h, target],
            send_sem=y_send.at[g], recv_sem=y_recv.at[g], device_id=inner, device_id_type=MESH,
        )

    def x_copy(turn_index, half, source, peer, lane):
        return pltpu.make_async_remote_copy(
            src_ref=panels.at[source, half], dst_ref=panels.at[turn_index, half],
            send_sem=x_send.at[lane, half], recv_sem=x_recv.at[turn_index - 1, half],
            device_id=peer, device_id_type=MESH,
        )

    def hop_copy(h, way):
        return pltpu.make_async_remote_copy(
            src_ref=stage.at[h, way], dst_ref=relay.at[h, way],
            send_sem=hop_send.at[h, way], recv_sem=hop_recv.at[h, way],
            device_id=(inner, outer)[way], device_id_type=MESH,
        )

    def last_copy(h, way):
        return pltpu.make_async_remote_copy(
            src_ref=relay.at[h, way], dst_ref=arrived.at[h, way],
            send_sem=last_send.at[h, way], recv_sem=last_recv.at[h, way],
            device_id=(outer, inner)[way], device_id_type=MESH,
        )

    load_right(0).wait()
    pack(0, 0)
    load_right(1).wait()
    pack(0, 1)
    pl.semaphore_wait(barrier, len(peers))

    @pl.when(even_row)
    def _():
        z_copy(0, 0, 4).start()
        z_copy(1, 1, 5).start()

    @pl.when(odd == 1)
    def _():
        y_copy(0, 0, 2).start()
        z_copy(0, 1, 5).start()
        y_copy(1, 1, 3).start()

    for slot in range(2):
        for half in range(2):
            load_left(slot, half).wait()

    near_slot = jnp.where(chip == 0, 4, 0)
    far_slot = jnp.where(chip < 2, 4, 0)
    for half in range(2):
        x_copy(2, half, near_slot, left, 0).start()

    @pl.when(even_core)
    def _():
        for half in range(2):
            x_copy(3, half, far_slot, far, 1).start()

    @pl.when(core == 1)
    def _():
        for half in range(2):
            x_copy(1, half, 0, sibling, 1).start()

    for h in range(1, STRIPS):
        for half in range(2):
            pack(h, half)

    sums[...] = jnp.zeros_like(sums)

    def fill_left(turn_index, half):
        def one(kk, carry):
            marks = panels[turn_index, half, pl.ds(HALF * LPB * BS, 8), :]
            at = pl.ds(pl.multiple_of(kk * BS, BS), BS)
            first = panels[turn_index, half, pl.ds(pl.multiple_of(kk * LPB * BS, BS), BS), :]
            second = panels[turn_index, half, pl.ds(pl.multiple_of(kk * LPB * BS + BS, BS), BS), :]
            mark_row = lambda e: jnp.sum(jnp.where(sub8 == e, marks, 0.0), axis=0, keepdims=True)
            first_row = jnp.broadcast_to(mark_row(kk * LPB), (BS, BS))
            second_row = jnp.broadcast_to(mark_row(kk * LPB + 1), (BS, BS))
            for r in range(RB):
                block = jnp.where(first_row == r, first, jnp.where(second_row == r, second, 0.0))
                hi = block.astype(bf16)
                left_hi[turn_index, half, r, :, at] = hi
                left_lo[turn_index, half, r, :, at] = (block - hi.astype(f32)).astype(bf16)
            return carry

        lax.fori_loop(0, HALF, one, 0)

    fill_left(0, 0)
    fill_left(0, 1)

    def products(h, unit):
        turn_index = lax.div(unit, 2)
        half = lax.rem(unit, 2)

        def fill(kk, carry):
            marks = units[h, unit, pl.ds(HALF * BS, 8), :]
            mine = jnp.sum(jnp.where(sub8 == kk, marks, 0.0), axis=0, keepdims=True)
            mine = jnp.broadcast_to(mine, (8, BS))
            at = pl.ds(pl.multiple_of(kk * BS, BS), BS)
            packed = units[h, unit, at, :]
            for u in range(2):
                total = None
                for turned in range(STRIPS):
                    place = jnp.broadcast_to(shifted(mine, STRIPS - turned)[:1], (BS, BS))
                    term = jnp.where(place == (group + 4 * u).astype(f32), shifted(packed, STRIPS - turned), 0.0)
                    total = term if total is None else total + term
                hi = total.astype(bf16)
                right_hi[at, u * BS:(u + 1) * BS] = hi
                right_lo[at, u * BS:(u + 1) * BS] = (total - hi.astype(f32)).astype(bf16)
            return carry

        lax.fori_loop(0, HALF, fill, 0)
        l_hi = left_hi[turn_index, half].reshape(RB * BS, HALF * BS)
        l_lo = left_lo[turn_index, half].reshape(RB * BS, HALF * BS)
        got = jnp.dot(l_hi, right_hi[...], preferred_element_type=f32)
        got += jnp.dot(l_lo, right_hi[...], preferred_element_type=f32)
        got += jnp.dot(l_hi, right_lo[...], preferred_element_type=f32)
        for u in range(2):
            for r in range(RB):
                sums[h * CB + u * RB + r] += got[r * BS:(r + 1) * BS, u * BS:(u + 1) * BS]

    def gather(h, first, keep):
        def one(q, carry):
            parts = []
            for b in range(STRIPS):
                slot = slots[first + q * STRIPS + b]
                r = lax.div(slot, CB)
                c = lax.rem(slot, CB)
                block = sums[h * CB + lax.div(c, 4) * RB + r]
                away = lax.rem(b - lax.rem(c, 4) + STRIPS, STRIPS)
                placed = block
                for groups in range(1, STRIPS):
                    placed = jnp.where(away == groups, shifted(block, groups), placed)
                parts.append(placed)
            whole = regroup(group, parts)
            keep[h, 0, q] = whole[:BS // 2]
            keep[h, 1, q] = whole[BS // 2:]
            return carry

        lax.fori_loop(0, PACKS, one, 0)

    def pass_on(h):
        for way in range(2):
            hop_copy(h, way).wait_recv()
            last_copy(h, way).start()

    def step(g, carry):
        h = lax.div(g, 3)
        s = lax.rem(g, 3)
        z_unit = 4 + s + odd
        y_unit = jnp.where(s < 2, 2 + s, 7 - 3 * odd)
        more = g < STAGES - 3

        z_copy(g, z_unit, z_unit).wait_recv()

        @pl.when(even_row)
        def _():
            y_copy(g, z_unit, 2 + s).start()

        @pl.when((odd == 1) & (s == 0))
        def _():
            y_copy(g + 2, z_unit, 7).start()

        y_copy(g, y_unit, y_unit).wait_recv()

        @pl.when(even_row & (s == 0))
        def _():
            z_copy(g + 2, y_unit, 6).start()

        @pl.when((odd == 1) & (s < 2))
        def _():
            z_copy(g + 1, y_unit, 6 + s).start()

        @pl.when(even_row & (s > 0) & more)
        def _():
            z_copy(g + 2, s - 1, 3 + s).start()

        @pl.when((odd == 1) & (s > 0) & more)
        def _():
            y_copy(g + 2, s - 1, 1 + s).start()

        @pl.when((odd == 1) & (s == 1) & more)
        def _():
            z_copy(g + 2, 1, 5).start()

        @pl.when(g == 4)
        def _():
            for half in range(2):
                x_copy(2, half, 0, left, 0).wait_recv()

            @pl.when(even_core)
            def _():
                for half in range(2):
                    x_copy(1, half, 2, sibling, 2).start()

            @pl.when(core == 1)
            def _():
                for half in range(2):
                    x_copy(3, half, 2, sibling, 2).start()

        @pl.when(g == 5)
        def _():
            for half in range(2):
                x_copy(1, half, 0, sibling, 1).wait_recv()
                x_copy(3, half, 0, sibling, 1).wait_recv()

            def one(i, c):
                fill_left(1 + lax.div(i, 2), lax.rem(i, 2))
                return c

            lax.fori_loop(0, 6, one, 0)

        for at, strip in ((7, 0), (9, 1), (10, 2)):
            @pl.when(g == at)
            def _():
                pass_on(strip)

        def done(at):
            late = jnp.where(at == 8, 24, jnp.where(at == 9, 28, 10 + 2 * at))
            return jnp.where(at < 2, at + 1, jnp.where(at < 5, 2, jnp.where(at < 8, 6 * at - 22, late)))

        start = done(g - 1)

        def task(i, c):
            q = start + i

            @pl.when(q < done(g))
            def _():
                th = lax.div(q, 8)
                j = lax.rem(q, 8)
                ts = lax.div(j + 6, 2) - 4
                from_z = 4 + ts + odd
                from_y = jnp.where(ts < 2, 2 + ts, 7 - 3 * odd)
                unit = jnp.where(j < 2, j, jnp.where(lax.rem(j, 2) == 0, from_z, from_y))
                products(th, unit)

            return c

        lax.fori_loop(0, 6, task, 0)

        @pl.when((g == 5) | (g == 7) | (g == 8) | (g == 11))
        def _():
            strip = jnp.where(g == 5, 0, jnp.where(g == 7, 1, jnp.where(g == 8, 2, 3)))
            gather(strip, OWNED * (1 - rep), stage)
            for way in range(2):
                hop_copy(strip, way).start()
            gather(strip, OWNED * rep, own)

        return carry

    lax.fori_loop(0, STAGES, step, 0)
    pass_on(STRIPS - 1)

    def finish_wait(h, carry):
        for way in range(2):
            last_copy(h, way).wait_recv()
        return carry

    lax.fori_loop(0, STRIPS, finish_wait, 0)
    group_half = group[:BS // 2]

    def finish(i, carry):
        q = lax.div(i, 2)
        way = lax.rem(i, 2)
        whole = [own[h, way, q] + arrived[h, way, q] for h in range(STRIPS)]
        at = pl.ds(pl.multiple_of(way * (BS // 2), BS // 2), BS // 2)
        for b in range(STRIPS):
            out[q * STRIPS + b, at, :] = regroup(group_half, [shifted(whole[h], h - b) for h in range(STRIPS)])
        return carry

    lax.fori_loop(0, 2 * PACKS, finish, 0)

    def z_sent(g, carry):
        z_copy(g, 0, 0).wait_send()
        y_copy(g, 0, 0).wait_send()
        return carry

    lax.fori_loop(0, STAGES, z_sent, 0)
    for lane in range(3):
        for half in range(2):
            x_lane_sent(x_copy, lane, half, left)
    for h in range(STRIPS):
        for way in range(2):
            hop_copy(h, way).wait_send()
            last_copy(h, way).wait_send()


def x_lane_sent(x_copy, lane, half, peer):
    x_copy(1, half, 0, peer, lane).wait_send()


def shards(rows, columns, left_values, left_rows, right_values, right_cols, result_slots):
    left = left_values.reshape(2, 2, HALF * LPB * BS, BS)
    right = right_values.reshape(KB * BPR, BS, BS)
    vmem = pltpu.VMEM
    dma = pltpu.SemaphoreType.DMA
    out = pl.pallas_call(
        functools.partial(kernel, rows, columns),
        out_shape=jax.ShapeDtypeStruct((OWNED, BS, BS), f32),
        in_specs=[
            pl.BlockSpec(memory_space=pl.ANY),
            pl.BlockSpec(memory_space=pl.ANY),
            pl.BlockSpec(memory_space=pltpu.SMEM),
            pl.BlockSpec(memory_space=pltpu.SMEM),
            pl.BlockSpec(memory_space=pltpu.SMEM),
        ],
        out_specs=pl.BlockSpec(memory_space=vmem),
        scratch_shapes=[
            vmem((KB * BPR, BS, BS), f32),
            vmem((STRIPS, 8, UNIT, BS), f32),
            vmem((5, 2, PANEL, BS), f32),
            vmem((4, 2, RB, BS, HALF * BS), bf16),
            vmem((4, 2, RB, BS, HALF * BS), bf16),
            vmem((HALF * BS, 2 * BS), bf16),
            vmem((HALF * BS, 2 * BS), bf16),
            vmem((STRIPS * CB, BS, BS), f32),
            vmem((STRIPS, 2, PACKS, BS // 2, BS), f32),
            vmem((STRIPS, 2, PACKS, BS // 2, BS), f32),
            vmem((STRIPS, 2, PACKS, BS // 2, BS), f32),
            vmem((STRIPS, 2, PACKS, BS // 2, BS), f32),
            dma((2,)), dma((2, 2)),
            dma((STAGES,)), dma((STAGES,)), dma((STAGES,)), dma((STAGES,)),
            dma((3, 2)), dma((3, 2)),
            dma((STRIPS, 2)), dma((STRIPS, 2)), dma((STRIPS, 2)), dma((STRIPS, 2)),
        ],
        compiler_params=pltpu.CompilerParams(
            collective_id=0, has_side_effects=True, vmem_limit_bytes=48 * 2**20
        ),
    )(left, right, left_rows.reshape(-1), right_cols.reshape(-1), result_slots.reshape(-1))
    return out[None, None]


def solution(mesh):
    in_specs = (
        P("row", "rep", "col", None, None, None, None, None),
        P("row", "rep", "col", None, None, None),
        P("rep", "row", "col", None, None, None, None),
        P("rep", "row", "col", None, None),
        P("row", "col", None),
    )
    out_specs = P("row", "col", "rep", None, None)
    body = functools.partial(shards, mesh.shape["row"], mesh.shape["col"])
    return jax.shard_map(body, mesh=mesh, in_specs=in_specs, out_specs=out_specs, check_vma=False)
```

```python
import functools

import jax
import jax.numpy as jnp
from jax import lax
from jax.experimental import pallas as pl
from jax.experimental.pallas import tpu as pltpu
from jax.sharding import PartitionSpec as P

BS = 128
KB = 8
BPR = 4
LPB = 2
RB = 4
CB = 8
NC = 24
STRIPS = 4
LANES = BS // STRIPS
OWNED = NC // 2
PACKS = OWNED // STRIPS
QUARTERS = 4
DEPTH = KB // QUARTERS * BS
TASKS = 4 * QUARTERS
SLAB = 32
VMEM_LIMIT = 60 * 2**20
MESH = pl.DeviceIdType.MESH
f32 = jnp.float32
bf16 = jnp.bfloat16

SLOT = {
    "zE0": (0, 0, 1), "zE1": (1, 1, 1), "zE2": (2, 2, 1), "zE3": (3, 3, 1), "zA": (4, 0, 1), "zB": (4, 1, 2), "zD": (5, 3, 1),
    "yE0": (0, 0, 1), "yE1": (1, 1, 1), "yE2": (2, 2, 1), "yE3": (3, 3, 1), "yA": (4, 0, 1),
    "oA": (0, 0, 1), "oB": (1, 1, 2), "oD": (2, 3, 1), "ob": (3, 1, 2),
}
WAITS = {
    0: [('zE0', 2), ('zE1', 2), ('zE2', 2), ('oA', 1), ('oD', 1), ('zE3', 2), ('zA', 3), ('oB', 1), ('zD', 3), ('ob', 3)],
    1: [('yE0', 1), ('yE1', 1), ('zB', 2), ('yE2', 1), ('yE3', 1), ('zE0', 3), ('zD', 2), ('zE2', 3), ('yA', 2), ('zE1', 3), ('zE3', 3)],
}
RELAYS = {
    0: {"zE0": ("yE0", 2, 1), "zE1": ("yE1", 2, 1), "zE2": ("yE2", 2, 1), "zE3": ("yE3", 2, 1),
        "zA": ("yA", 3, 2), "oA": ("zA", 1, 3), "oD": ("zD", 1, 3)},
    1: {"zB": ("ob", 2, 3), "yE0": ("zE0", 1, 3), "yE1": ("zE1", 1, 3), "yE2": ("zE2", 1, 3), "yE3": ("zE3", 1, 3)},
}
OWN = {
    0: [('zE0', 2, 0), ('zE1', 2, 4), ('zE2', 2, 6), ('zE3', 2, 9)],
    1: [('oD', 1, 1), ('zD', 2, 3), ('zB', 2, 4), ('oA', 1, 4), ('oB', 1, 5)],
}
STEPS = 11
PASS_ON = {0: [31, 40, 39], 1: [36, 31, 36]}
LEFT_RELAY = {0: 14, 1: 14}
LEFT_READY = {0: 17, 1: 17}
DONE = {
    0: [1, 2, 3, 4, 4, 4, 4, 4, 4, 4, 4, 4, 4, 4, 4, 4, 4, 6, 8, 10, 12, 12, 15, 18, 21, 24, 27, 30, 33, 36, 39, 42, 42, 45, 48, 51, 54, 57, 58, 59, 61, 62, 64, 64],
    1: [1, 2, 3, 4, 4, 4, 4, 4, 4, 4, 4, 4, 4, 4, 4, 4, 4, 7, 10, 13, 16, 19, 22, 25, 28, 31, 34, 37, 40, 43, 46, 47, 48, 50, 52, 54, 56, 58, 59, 60, 61, 62, 63, 64],
}
ORDER = {
    0: [0, 1, 2, 3, 8, 9, 10, 4, 7, 11, 12, 5, 6, 15, 13, 14],
    1: [0, 1, 2, 3, 4, 5, 9, 10, 6, 7, 12, 11, 14, 8, 13, 15],
}
MOST = max(b - a for role in (0, 1) for a, b in zip([0] + DONE[role], DONE[role]))


def by_role(odd, even_value, odd_value):
    return even_value + odd * (odd_value - even_value)


def lookup(index, values):
    found = jnp.int32(values[0])
    for at in range(1, len(values)):
        if values[at] != values[at - 1]:
            found = found + jnp.where(index >= at, values[at] - values[at - 1], 0)
    return found


def regroup(group, parts):
    picked = parts[STRIPS - 1]
    for b in range(STRIPS - 2, -1, -1):
        picked = jnp.where(group == b, parts[b], picked)
    return picked


def shifted(x, groups):
    by = (groups * LANES) % BS
    return x if by == 0 else pltpu.roll(x, by, 1)


def sum_of_dots(left_parts, right_parts, turn_index, quarter):
    left = jnp.concatenate([left_parts[turn_index, quarter, part] for part in range(3)], axis=1)
    right = right_parts[...].reshape(3 * DEPTH, 2 * BS)
    return jnp.dot(left, right, preferred_element_type=f32)


def kernel(
    rows, columns,
    left_hbm, right_hbm, left_rows_hbm, right_cols_hbm, slots_hbm, out,
    raw, units, panels, left_parts, right_parts, sums,
    own, stage, relay, arrived, marks, wheres, left_rows, right_cols, slots,
    load_sem, left_load_sem, small_sem, z_send, z_recv, y_send, y_recv, x_send, x_recv,
    mark_send, mark_recv, hop_send, hop_recv, last_send, last_recv,
):
    row = lax.axis_index("row")
    col = lax.axis_index("col")
    rep = lax.axis_index("rep")
    odd = lax.rem(row, 2)
    core = lax.rem(col, 2)
    chip = lax.div(col, 2)
    is_role = {0: odd == 0, 1: odd == 1}
    mate_row = row + 1 - 2 * odd
    up = (lax.rem(row + 2, rows), col, rep)
    down = (lax.rem(row + rows - 2, rows), col, rep)
    inner = (mate_row, col, rep)
    outer = (mate_row, col, 1 - rep)
    sibling = (row, col + 1 - 2 * core, rep)
    right = (row, lax.rem(col + 2, columns), rep)
    left = (row, lax.rem(col + columns - 2, columns), rep)
    far = (row, lax.rem(col - core + 4, columns) + 1 - core, rep)

    barrier = pltpu.get_barrier_semaphore()
    peers = (up, down, inner, outer, sibling, right, left, far)
    for peer in peers:
        pl.semaphore_signal(barrier, inc=1, device_id=peer, device_id_type=MESH)

    small = [
        pltpu.make_async_copy(right_cols_hbm, right_cols, small_sem.at[0]),
        pltpu.make_async_copy(left_rows_hbm, left_rows, small_sem.at[1]),
        pltpu.make_async_copy(slots_hbm, slots, small_sem.at[2]),
    ]

    def load_right(half):
        part = pl.ds(half * KB * BPR // 2, KB * BPR // 2)
        return pltpu.make_async_copy(right_hbm.at[part], raw.at[part], load_sem.at[half])

    def load_left(slot):
        return pltpu.make_async_copy(
            left_hbm.at[slot], panels.at[4 * slot, pl.ds(0, KB * LPB * BS)], left_load_sem.at[slot]
        )

    small[0].start()
    for half in range(2):
        load_right(half).start()
    small[1].start()
    small[2].start()
    for slot in range(2):
        load_left(slot).start()

    group = lax.broadcasted_iota(jnp.int32, (SLAB, BS), 1) // LANES
    sub8 = lax.broadcasted_iota(jnp.int32, (8, BS), 0)
    group8 = lax.broadcasted_iota(jnp.int32, (8, BS), 1) // LANES

    def pack(h, k):
        for slab in range(0, BS, SLAB):
            parts = [shifted(raw[k * BPR + b, pl.ds(slab, SLAB), :], b - h) for b in range(BPR)]
            at = pl.ds(pl.multiple_of(lax.rem(k, 2) * BS + slab, SLAB), SLAB)
            units[h, lax.div(k, 2), at, :] = regroup(group, parts)

    def unit_copy(link, name, h, source, target):
        slot, first, count = SLOT[name]
        sends, recvs, peer = (z_send, z_recv, down) if link == "z" else (y_send, y_recv, inner)
        return pltpu.make_async_remote_copy(
            src_ref=units.at[h, pl.ds(source * QUARTERS + first, count)],
            dst_ref=units.at[h, pl.ds(target * QUARTERS + first, count)],
            send_sem=sends.at[h, slot], recv_sem=recvs.at[h, slot], device_id=peer, device_id_type=MESH,
        )

    def link_of(name):
        return "z" if name[0] == "z" else "y"

    def x_copy(turn_index, source, peer, lane):
        return pltpu.make_async_remote_copy(
            src_ref=panels.at[source], dst_ref=panels.at[turn_index],
            send_sem=x_send.at[lane], recv_sem=x_recv.at[turn_index - 1],
            device_id=peer, device_id_type=MESH,
        )

    def mark_copy(source, target, peer, lane):
        return pltpu.make_async_remote_copy(
            src_ref=marks.at[source], dst_ref=marks.at[target],
            send_sem=mark_send.at[lane], recv_sem=mark_recv.at[target - 1],
            device_id=peer, device_id_type=MESH,
        )

    def hop_copy(h, way):
        return pltpu.make_async_remote_copy(
            src_ref=stage.at[h, way], dst_ref=relay.at[h, way],
            send_sem=hop_send.at[h, way], recv_sem=hop_recv.at[h, way],
            device_id=(inner, outer)[way], device_id_type=MESH,
        )

    def last_copy(h, way):
        return pltpu.make_async_remote_copy(
            src_ref=relay.at[h, way], dst_ref=arrived.at[h, way],
            send_sem=last_send.at[h, way], recv_sem=last_recv.at[h, way],
            device_id=(outer, inner)[way], device_id_type=MESH,
        )

    small[0].wait()
    places = jnp.zeros((8, BS), f32)
    for b in range(BPR):
        for k in range(KB):
            places = jnp.where((group8 == b) & (sub8 == k), right_cols[b, k].astype(f32), places)
    marks[0] = places

    def pack_first(k, carry):
        pack(0, k)
        return carry

    for half in range(2):
        load_right(half).wait()
        lax.fori_loop(half * KB // 2, (half + 1) * KB // 2, pack_first, 0)
    pl.semaphore_wait(barrier, len(peers))

    for role in (0, 1):
        @pl.when(is_role[role])
        def _():
            if role == 0:
                mark_copy(0, 2, down, 0).start()
            else:
                mark_copy(0, 1, inner, 0).start()
                mark_copy(0, 2, down, 1).start()
            for name, target, _ in OWN[role]:
                unit_copy(link_of(name), name, 0, 0, target).start()

    small[1].wait()
    for slot in range(2):
        load_left(slot).wait()
        for a in range(LPB):
            places = jnp.zeros((8, BS), f32)
            for k in range(KB):
                places = jnp.where(sub8 == k, left_rows[slot, a, k].astype(f32), places)
            panels[4 * slot, pl.ds(KB * LPB * BS + 8 * a, 8), :] = places

    x_copy(2, jnp.where(chip == 0, 4, 0), left, 0).start()

    @pl.when(core == 0)
    def _():
        x_copy(3, jnp.where(chip < 2, 4, 0), far, 1).start()

    @pl.when(core == 1)
    def _():
        x_copy(1, 0, sibling, 1).start()

    def pack_rest(k, carry):
        for h in range(1, STRIPS):
            pack(h, k)
        return carry

    lax.fori_loop(0, KB, pack_rest, 0)
    sums[...] = jnp.zeros_like(sums)
    small[2].wait()

    def row_of(tile, k):
        one = jnp.sum(jnp.where(sub8 == k, tile, 0.0), axis=0, keepdims=True)
        return jnp.broadcast_to(one, (8, BS))

    def tall(x):
        return x.reshape(SLAB // 8, 8, BS)

    def fill_left(turn_index):
        def one(k, carry):
            quarter = lax.div(k, 2)
            at = pl.ds(pl.multiple_of(lax.rem(k, 2) * BS, BS), BS)
            where = [row_of(panels[turn_index, pl.ds(KB * LPB * BS + 8 * a, 8), :], k) for a in range(LPB)]
            for slab in range(0, BS, SLAB):
                blocks = [
                    tall(panels[turn_index, pl.ds(pl.multiple_of((k * LPB + a) * BS + slab, SLAB), SLAB), :])
                    for a in range(LPB)
                ]
                for r in range(RB):
                    second = jnp.where((where[1] == r)[None], blocks[1], 0.0)
                    block = jnp.where((where[0] == r)[None], blocks[0], second).reshape(SLAB, BS)
                    hi = block.astype(bf16)
                    lo = (block - hi.astype(f32)).astype(bf16)
                    for part, value in enumerate((hi, lo, hi)):
                        left_parts[turn_index, quarter, part, pl.ds(r * BS + slab, SLAB), at] = value
            return carry

        lax.fori_loop(0, KB, one, 0)

    def fill_wheres(turn_index):
        tile = marks[turn_index]
        for k in range(KB):
            mine = row_of(tile, k)
            for turned in range(STRIPS):
                wheres[turn_index, k, turned] = shifted(mine, STRIPS - turned)

    fill_left(0)
    fill_wheres(0)

    def products(h, turn_index, quarter):
        for kk in range(KB // QUARTERS):
            places = [wheres[turn_index, quarter * 2 + kk, turned] for turned in range(STRIPS)]
            masks = [[(place == (group8 + 4 * u).astype(f32))[None] for place in places] for u in range(2)]
            for slab in range(0, BS, SLAB):
                at = pl.ds(kk * BS + slab, SLAB)
                packed = units[h, turn_index * QUARTERS + quarter, at, :]
                blocks = [tall(shifted(packed, STRIPS - turned)) for turned in range(STRIPS)]
                for u in range(2):
                    terms = [jnp.where(mask, block, 0.0) for mask, block in zip(masks[u], blocks)]
                    whole = ((terms[0] + terms[1]) + (terms[2] + terms[3])).reshape(SLAB, BS)
                    hi = whole.astype(bf16)
                    lo = (whole - hi.astype(f32)).astype(bf16)
                    for part, value in enumerate((hi, hi, lo)):
                        right_parts[part, at, u * BS:(u + 1) * BS] = value
        got = sum_of_dots(left_parts, right_parts, turn_index, quarter)
        for u in range(2):
            for r in range(RB):
                sums[h * CB + u * RB + r] += got[r * BS:(r + 1) * BS, u * BS:(u + 1) * BS]

    def gather(h, first, keep):
        def one(q, carry):
            found = []
            for b in range(STRIPS):
                slot = slots[0, first + q * STRIPS + b]
                c = lax.rem(slot, CB)
                away = lax.rem(b - lax.rem(c, 4) + STRIPS, STRIPS)
                found.append((h * CB + lax.div(c, 4) * RB + lax.div(slot, CB), away * LANES))
            for slab in range(0, BS, SLAB):
                parts = [pltpu.roll(sums[block, pl.ds(slab, SLAB), :], by, 1) for block, by in found]
                way, at = divmod(slab, BS // 2)
                keep[h, way, q, pl.ds(at, SLAB), :] = regroup(group, parts)
            return carry

        lax.fori_loop(0, PACKS, one, 0)

    def pass_on(h):
        for way in range(2):
            hop_copy(h, way).wait_recv()
            last_copy(h, way).start()

    def step(g, carry):
        h = lax.div(g, STEPS)
        s = lax.rem(g, STEPS)
        for role in (0, 1):
            for at, (name, turn_index) in enumerate(WAITS[role]):
                @pl.when(is_role[role] & (s == at))
                def _():
                    unit_copy(link_of(name), name, h, turn_index, turn_index).wait_recv()
                    sent_on = RELAYS[role].get(name)
                    if sent_on is not None:
                        unit_copy(link_of(sent_on[0]), sent_on[0], h, sent_on[1], sent_on[2]).start()
                    if role == 0 and name == "zE0":
                        @pl.when(h == 0)
                        def _():
                            mark_copy(0, 2, inner, 0).wait_recv()
                            mark_copy(2, 1, inner, 1).start()
                    if role == 1 and name == "yE0":
                        @pl.when(h == 0)
                        def _():
                            mark_copy(0, 1, inner, 0).wait_recv()
                            mark_copy(1, 3, down, 2).start()
                    if role == 1 and name == "zB":
                        @pl.when(h == 0)
                        def _():
                            mark_copy(0, 2, inner, 0).wait_recv()
                            mark_copy(2, 3, inner, 3).start()

                    @pl.when(h < STRIPS - 1)
                    def _():
                        for own_name, target, after in OWN[role]:
                            if after == at:
                                unit_copy(link_of(own_name), own_name, h + 1, 0, target).start()

        @pl.when(g == by_role(odd, LEFT_RELAY[0], LEFT_RELAY[1]))
        def _():
            x_copy(2, 0, left, 0).wait_recv()

            @pl.when(core == 0)
            def _():
                x_copy(1, 2, sibling, 2).start()

            @pl.when(core == 1)
            def _():
                x_copy(3, 2, sibling, 2).start()

        @pl.when(g == by_role(odd, LEFT_READY[0], LEFT_READY[1]))
        def _():
            x_copy(1, 0, sibling, 1).wait_recv()
            x_copy(3, 0, sibling, 1).wait_recv()
            for role in (0, 1):
                @pl.when(is_role[role])
                def _():
                    for turn_index in ((1, 3), (3,))[role]:
                        mark_copy(0, turn_index, inner, 0).wait_recv()

            def one(i, c):
                fill_left(i)
                fill_wheres(i)
                return c

            lax.fori_loop(1, 4, one, 0)

        for strip in range(STRIPS - 1):
            @pl.when(g == by_role(odd, PASS_ON[0][strip], PASS_ON[1][strip]))
            def _():
                pass_on(strip)

        before = by_role(odd, lookup(g, [0] + DONE[0]), lookup(g, [0] + DONE[1]))
        after = by_role(odd, lookup(g, DONE[0]), lookup(g, DONE[1]))

        def task(i, c):
            q = before + i

            @pl.when(q < after)
            def _():
                j = lax.rem(q, TASKS)
                code = by_role(odd, lookup(j, ORDER[0]), lookup(j, ORDER[1]))
                products(lax.div(q, TASKS), lax.div(code, QUARTERS), lax.rem(code, QUARTERS))

            return c

        lax.fori_loop(0, MOST, task, 0)

        @pl.when(lax.div(after, TASKS) > lax.div(before, TASKS))
        def _():
            strip = lax.div(before, TASKS)
            gather(strip, OWNED * (1 - rep), stage)
            for way in range(2):
                hop_copy(strip, way).start()
            gather(strip, OWNED * rep, own)

        return carry

    lax.fori_loop(0, STRIPS * STEPS, step, 0)
    pass_on(STRIPS - 1)

    def finish_wait(h, carry):
        for way in range(2):
            last_copy(h, way).wait_recv()
        return carry

    lax.fori_loop(0, STRIPS, finish_wait, 0)

    def finish(i, carry):
        q = lax.div(i, 2)
        way = lax.rem(i, 2)
        for slab in range(0, BS // 2, SLAB):
            part = pl.ds(slab, SLAB)
            whole = [own[h, way, q, part, :] + arrived[h, way, q, part, :] for h in range(STRIPS)]
            at = pl.ds(pl.multiple_of(way * (BS // 2) + slab, SLAB), SLAB)
            for b in range(STRIPS):
                out[q * STRIPS + b, at, :] = regroup(group, [shifted(whole[h], h - b) for h in range(STRIPS)])
        return carry

    lax.fori_loop(0, 2 * PACKS, finish, 0)

    def sent(h, carry):
        for role in (0, 1):
            @pl.when(is_role[role])
            def _():
                names = [name for name, _, _ in RELAYS[role].values()] + [name for name, _, _ in OWN[role]]
                for name in names:
                    unit_copy(link_of(name), name, h, 0, 0).wait_send()

        for way in range(2):
            hop_copy(h, way).wait_send()
            last_copy(h, way).wait_send()
        return carry

    lax.fori_loop(0, STRIPS, sent, 0)
    for role in (0, 1):
        @pl.when(is_role[role])
        def _():
            for lane in range((2, 4)[role]):
                mark_copy(0, 1, inner, lane).wait_send()
    for lane in range(3):
        x_copy(1, 0, left, lane).wait_send()


def shards(rows, columns, left_values, left_rows, right_values, right_cols, result_slots):
    left = left_values.reshape(2, KB * LPB * BS, BS)
    right = right_values.reshape(KB * BPR, BS, BS)
    vmem = pltpu.VMEM
    dma = pltpu.SemaphoreType.DMA
    out = pl.pallas_call(
        functools.partial(kernel, rows, columns),
        out_shape=jax.ShapeDtypeStruct((OWNED, BS, BS), f32),
        in_specs=[pl.BlockSpec(memory_space=pltpu.HBM)] * 5,
        out_specs=pl.BlockSpec(memory_space=vmem),
        scratch_shapes=[
            vmem((KB * BPR, BS, BS), f32),
            vmem((STRIPS, 4 * QUARTERS, DEPTH, BS), f32),
            vmem((5, KB * LPB * BS + 16, BS), f32),
            vmem((4, QUARTERS, 3, RB * BS, DEPTH), bf16),
            vmem((3, DEPTH, 2 * BS), bf16),
            vmem((STRIPS * CB, BS, BS), f32),
            vmem((STRIPS, 2, PACKS, BS // 2, BS), f32),
            vmem((STRIPS, 2, PACKS, BS // 2, BS), f32),
            vmem((STRIPS, 2, PACKS, BS // 2, BS), f32),
            vmem((STRIPS, 2, PACKS, BS // 2, BS), f32),
            vmem((4, 8, BS), f32),
            vmem((4, KB, STRIPS, 8, BS), f32),
            pltpu.SMEM((2, LPB, KB), jnp.int32),
            pltpu.SMEM((BPR, KB), jnp.int32),
            pltpu.SMEM((1, NC), jnp.int32),
            dma((2,)), dma((2,)), dma((3,)),
            dma((STRIPS, 6)), dma((STRIPS, 6)), dma((STRIPS, 5)), dma((STRIPS, 5)),
            dma((3,)), dma((3,)), dma((4,)), dma((3,)),
            dma((STRIPS, 2)), dma((STRIPS, 2)), dma((STRIPS, 2)), dma((STRIPS, 2)),
        ],
        compiler_params=pltpu.CompilerParams(
            collective_id=0, has_side_effects=True, vmem_limit_bytes=VMEM_LIMIT
        ),
    )(
        left, right, left_rows.reshape(2, KB, LPB).transpose(0, 2, 1), right_cols.reshape(KB, BPR).T,
        result_slots.reshape(1, NC),
    )
    return out[None, None]


def solution(mesh):
    in_specs = (
        P("row", "rep", "col", None, None, None, None, None),
        P("row", "rep", "col", None, None, None),
        P("rep", "row", "col", None, None, None, None),
        P("rep", "row", "col", None, None),
        P("row", "col", None),
    )
    out_specs = P("row", "col", "rep", None, None)
    body = functools.partial(shards, mesh.shape["row"], mesh.shape["col"])
    return jax.shard_map(body, mesh=mesh, in_specs=in_specs, out_specs=out_specs, check_vma=False)
```

```python
import functools

import jax
import jax.numpy as jnp
from jax import lax
from jax.experimental import pallas as pl
from jax.experimental.pallas import tpu as pltpu
from jax.sharding import PartitionSpec as P

BS = 128
KB = 8
BPR = 4
LPB = 2
RB = 4
CB = 8
NC = 24
STRIPS = 4
LANES = BS // STRIPS
OWNED = NC // 2
PACKS = OWNED // STRIPS
HALVES = 2
HALF = KB // HALVES
TASKS = 4 * HALVES
SLAB = 32
VMEM_LIMIT = 60 * 2**20
MESH = pl.DeviceIdType.MESH
f32 = jnp.float32
bf16 = jnp.bfloat16

IN_A = 2
IN_B = 4
SLOT = {
    "zE0": (0, 0, 2), "zE1": (1, 2, 2), "zE2": (2, 4, 2), "zE3": (3, 6, 2), "zA": (4, 0, IN_A), "zB": (4, IN_A, IN_B),
    "zD": (5, IN_A + IN_B, KB - IN_A - IN_B),
    "yE0": (0, 0, 2), "yE1": (1, 2, 2), "yE2": (2, 4, 2), "yE3": (3, 6, 2), "yA": (4, 0, IN_A),
    "oA": (0, 0, IN_A), "oB": (1, IN_A, IN_B), "oD": (2, IN_A + IN_B, KB - IN_A - IN_B), "ob": (3, IN_A, IN_B),
}
WAITS = {
    0: [('zE0', 2), ('zE1', 2), ('oA', 1), ('oD', 1), ('zE2', 2), ('zE3', 2), ('zA', 3), ('oB', 1), ('zD', 3), ('ob', 3)],
    1: [('yE0', 1), ('zB', 2), ('yE1', 1), ('yE2', 1), ('zD', 2), ('yE3', 1), ('zE0', 3), ('yA', 2), ('zE2', 3), ('zE1', 3), ('zE3', 3)],
}
RELAYS = {
    0: {"zE0": ("yE0", 2, 1), "zE1": ("yE1", 2, 1), "zE2": ("yE2", 2, 1), "zE3": ("yE3", 2, 1),
        "zA": ("yA", 3, 2), "oA": ("zA", 1, 3), "oD": ("zD", 1, 3)},
    1: {"zB": ("ob", 2, 3), "yE0": ("zE0", 1, 3), "yE1": ("zE1", 1, 3), "yE2": ("zE2", 1, 3), "yE3": ("zE3", 1, 3)},
}
OWN = {
    0: [('zE0', 2, 4), ('zE1', 2, 5), ('zE2', 2, 8), ('zE3', 2, 8)],
    1: [('zB', 2, 5), ('oA', 1, 6), ('oD', 1, 6), ('oB', 1, 7), ('zD', 2, 10)],
}
STEPS = 11
PASS_ON = {0: [42, 42, 40], 1: [35, 36, 35]}
LEFT_RELAY = {0: 14, 1: 14}
LEFT_READY = {0: 17, 1: 17}
DONE = {
    0: [1, 2, 2, 2, 2, 2, 2, 2, 2, 2, 2, 2, 2, 2, 2, 2, 2, 4, 6, 8, 10, 10, 11, 12, 13, 14, 15, 16, 17, 18, 19, 20, 20, 23, 26, 27, 27, 27, 28, 28, 30, 30, 32, 32],
    1: [2, 2, 2, 2, 2, 2, 2, 2, 2, 2, 2, 2, 2, 2, 2, 2, 2, 4, 6, 8, 10, 12, 13, 14, 15, 16, 17, 18, 19, 20, 21, 22, 23, 25, 26, 27, 27, 28, 29, 29, 30, 30, 31, 32],
}
ORDER = {
    0: [0, 1, 4, 5, 2, 3, 6, 7],
    1: [0, 1, 2, 5, 3, 4, 6, 7],
}
MOST = max(b - a for role in (0, 1) for a, b in zip([0] + DONE[role], DONE[role]))


def by_role(odd, even_value, odd_value):
    return even_value + odd * (odd_value - even_value)


def lookup(index, values):
    found = jnp.int32(values[0])
    for at in range(1, len(values)):
        if values[at] != values[at - 1]:
            found = found + jnp.where(index >= at, values[at] - values[at - 1], 0)
    return found


def regroup(group, parts):
    picked = parts[STRIPS - 1]
    for b in range(STRIPS - 2, -1, -1):
        picked = jnp.where(group == b, parts[b], picked)
    return picked


def shifted(x, groups):
    by = (groups * LANES) % BS
    return x if by == 0 else pltpu.roll(x, by, 1)


def kernel(
    rows, columns,
    left_hbm, right_hbm, left_rows_hbm, right_cols_hbm, slots_hbm, out,
    raw, units, panels, left_parts, right_first, right_second, sums,
    own, stage, relay, arrived, marks, wheres, left_rows, right_cols, slots,
    load_sem, left_load_sem, small_sem, z_send, z_recv, y_send, y_recv, x_send, x_recv,
    mark_send, mark_recv, hop_send, hop_recv, last_send, last_recv,
):
    row = lax.axis_index("row")
    col = lax.axis_index("col")
    rep = lax.axis_index("rep")
    odd = lax.rem(row, 2)
    core = lax.rem(col, 2)
    chip = lax.div(col, 2)
    is_role = {0: odd == 0, 1: odd == 1}
    mate_row = row + 1 - 2 * odd
    up = (lax.rem(row + 2, rows), col, rep)
    down = (lax.rem(row + rows - 2, rows), col, rep)
    inner = (mate_row, col, rep)
    outer = (mate_row, col, 1 - rep)
    sibling = (row, col + 1 - 2 * core, rep)
    right = (row, lax.rem(col + 2, columns), rep)
    left = (row, lax.rem(col + columns - 2, columns), rep)
    far = (row, lax.rem(col - core + 4, columns) + 1 - core, rep)

    barrier = pltpu.get_barrier_semaphore()
    peers = (up, down, inner, outer, sibling, right, left, far)
    for peer in peers:
        pl.semaphore_signal(barrier, inc=1, device_id=peer, device_id_type=MESH)

    small = [
        pltpu.make_async_copy(right_cols_hbm, right_cols, small_sem.at[0]),
        pltpu.make_async_copy(left_rows_hbm, left_rows, small_sem.at[1]),
        pltpu.make_async_copy(slots_hbm, slots, small_sem.at[2]),
    ]

    def load_right(half):
        part = pl.ds(half * KB * BPR // 2, KB * BPR // 2)
        return pltpu.make_async_copy(right_hbm.at[part], raw.at[part], load_sem.at[half])

    def load_left(slot):
        return pltpu.make_async_copy(
            left_hbm.at[slot], panels.at[4 * slot, pl.ds(0, KB * LPB * BS)], left_load_sem.at[slot]
        )

    small[0].start()
    for half in range(2):
        load_right(half).start()
    small[1].start()
    small[2].start()
    for slot in range(2):
        load_left(slot).start()

    group = lax.broadcasted_iota(jnp.int32, (SLAB, BS), 1) // LANES
    sub8 = lax.broadcasted_iota(jnp.int32, (8, BS), 0)
    group8 = lax.broadcasted_iota(jnp.int32, (8, BS), 1) // LANES

    def pack(h, k):
        for slab in range(0, BS, SLAB):
            parts = [shifted(raw[k * BPR + b, pl.ds(slab, SLAB), :], b - h) for b in range(BPR)]
            units[h, 0, pl.ds(pl.multiple_of(k * BS + slab, SLAB), SLAB), :] = regroup(group, parts)

    def unit_copy(link, name, h, source, target):
        slot, first, count = SLOT[name]
        sends, recvs, peer = (z_send, z_recv, down) if link == "z" else (y_send, y_recv, inner)
        return pltpu.make_async_remote_copy(
            src_ref=units.at[h, source, pl.ds(first * BS, count * BS)],
            dst_ref=units.at[h, target, pl.ds(first * BS, count * BS)],
            send_sem=sends.at[h, slot], recv_sem=recvs.at[h, slot], device_id=peer, device_id_type=MESH,
        )

    def link_of(name):
        return "z" if name[0] == "z" else "y"

    def x_copy(turn_index, source, peer, lane):
        return pltpu.make_async_remote_copy(
            src_ref=panels.at[source], dst_ref=panels.at[turn_index],
            send_sem=x_send.at[lane], recv_sem=x_recv.at[turn_index - 1],
            device_id=peer, device_id_type=MESH,
        )

    def mark_copy(source, target, peer, lane):
        return pltpu.make_async_remote_copy(
            src_ref=marks.at[source], dst_ref=marks.at[target],
            send_sem=mark_send.at[lane], recv_sem=mark_recv.at[target - 1],
            device_id=peer, device_id_type=MESH,
        )

    def hop_copy(h, way):
        return pltpu.make_async_remote_copy(
            src_ref=stage.at[h, way], dst_ref=relay.at[h, way],
            send_sem=hop_send.at[h, way], recv_sem=hop_recv.at[h, way],
            device_id=(inner, outer)[way], device_id_type=MESH,
        )

    def last_copy(h, way):
        return pltpu.make_async_remote_copy(
            src_ref=relay.at[h, way], dst_ref=arrived.at[h, way],
            send_sem=last_send.at[h, way], recv_sem=last_recv.at[h, way],
            device_id=(outer, inner)[way], device_id_type=MESH,
        )

    small[0].wait()
    places = jnp.zeros((8, BS), f32)
    for b in range(BPR):
        for k in range(KB):
            places = jnp.where((group8 == b) & (sub8 == k), right_cols[b, k].astype(f32), places)
    marks[0] = places

    def pack_first(k, carry):
        pack(0, k)
        return carry

    for half in range(2):
        load_right(half).wait()
        lax.fori_loop(half * KB // 2, (half + 1) * KB // 2, pack_first, 0)
    pl.semaphore_wait(barrier, len(peers))

    for role in (0, 1):
        @pl.when(is_role[role])
        def _():
            if role == 0:
                mark_copy(0, 2, down, 0).start()
            else:
                mark_copy(0, 1, inner, 0).start()
                mark_copy(0, 2, down, 1).start()
            for name, target, _ in OWN[role]:
                unit_copy(link_of(name), name, 0, 0, target).start()

    small[1].wait()
    for slot in range(2):
        load_left(slot).wait()
        for a in range(LPB):
            places = jnp.zeros((8, BS), f32)
            for k in range(KB):
                places = jnp.where(sub8 == k, left_rows[slot, a, k].astype(f32), places)
            panels[4 * slot, pl.ds(KB * LPB * BS + 8 * a, 8), :] = places

    x_copy(2, jnp.where(chip == 0, 4, 0), left, 0).start()

    @pl.when(core == 0)
    def _():
        x_copy(3, jnp.where(chip < 2, 4, 0), far, 1).start()

    @pl.when(core == 1)
    def _():
        x_copy(1, 0, sibling, 1).start()

    def pack_rest(k, carry):
        for h in range(1, STRIPS):
            pack(h, k)
        return carry

    lax.fori_loop(0, KB, pack_rest, 0)
    sums[...] = jnp.zeros_like(sums)
    small[2].wait()

    def row_of(tile, k):
        one = jnp.sum(jnp.where(sub8 == k, tile, 0.0), axis=0, keepdims=True)
        return jnp.broadcast_to(one, (8, BS))

    def tall(x):
        return x.reshape(SLAB // 8, 8, BS)

    def fill_left(turn_index):
        def one(k, carry):
            half = lax.div(k, HALF)
            at = pl.ds(pl.multiple_of(lax.rem(k, HALF) * BS, BS), BS)
            where = [row_of(panels[turn_index, pl.ds(KB * LPB * BS + 8 * a, 8), :], k) for a in range(LPB)]
            for slab in range(0, BS, SLAB):
                blocks = [
                    tall(panels[turn_index, pl.ds(pl.multiple_of((k * LPB + a) * BS + slab, SLAB), SLAB), :])
                    for a in range(LPB)
                ]
                for r in range(RB):
                    second = jnp.where((where[1] == r)[None], blocks[1], 0.0)
                    block = jnp.where((where[0] == r)[None], blocks[0], second).reshape(SLAB, BS)
                    hi = block.astype(bf16)
                    lo = (block - hi.astype(f32)).astype(bf16)
                    for part, value in enumerate((hi, lo)):
                        left_parts[turn_index, half, part, pl.ds(r * BS + slab, SLAB), at] = value
            return carry

        lax.fori_loop(0, KB, one, 0)

    def fill_wheres(turn_index):
        tile = marks[turn_index]
        for k in range(KB):
            mine = row_of(tile, k)
            for turned in range(STRIPS):
                wheres[turn_index, k, turned] = shifted(mine, STRIPS - turned)

    fill_left(0)
    fill_wheres(0)

    def products(h, turn_index, half):
        got = None
        depth = HALF * BS // 2
        for pair, right_parts in enumerate((right_first, right_second)):
            for kk in range(2):
                k = half * HALF + pair * 2 + kk
                places = [wheres[turn_index, k, turned] for turned in range(STRIPS)]
                masks = [[(place == (group8 + 4 * u).astype(f32))[None] for place in places] for u in range(2)]
                for slab in range(0, BS, SLAB):
                    packed = units[h, turn_index, pl.ds(pl.multiple_of(k * BS + slab, SLAB), SLAB), :]
                    blocks = [tall(shifted(packed, STRIPS - turned)) for turned in range(STRIPS)]
                    at = pl.ds(kk * BS + slab, SLAB)
                    for u in range(2):
                        terms = [jnp.where(mask, block, 0.0) for mask, block in zip(masks[u], blocks)]
                        whole = ((terms[0] + terms[1]) + (terms[2] + terms[3])).reshape(SLAB, BS)
                        hi = whole.astype(bf16)
                        right_parts[0, at, u * BS:(u + 1) * BS] = hi
                        right_parts[1, at, u * BS:(u + 1) * BS] = (whole - hi.astype(f32)).astype(bf16)
        for pair, right_parts in enumerate((right_first, right_second)):
            for left_part, right_part in ((0, 0), (1, 0), (0, 1)):
                mine = left_parts[turn_index, half, left_part, :, pair * depth:(pair + 1) * depth]
                term = jnp.dot(mine, right_parts[right_part], preferred_element_type=f32)
                got = term if got is None else got + term
        for u in range(2):
            for r in range(RB):
                sums[h * CB + u * RB + r] += got[r * BS:(r + 1) * BS, u * BS:(u + 1) * BS]

    def gather(h, first, keep):
        def one(q, carry):
            found = []
            for b in range(STRIPS):
                slot = slots[0, first + q * STRIPS + b]
                c = lax.rem(slot, CB)
                away = lax.rem(b - lax.rem(c, 4) + STRIPS, STRIPS)
                found.append((h * CB + lax.div(c, 4) * RB + lax.div(slot, CB), away * LANES))
            for slab in range(0, BS, SLAB):
                parts = [pltpu.roll(sums[block, pl.ds(slab, SLAB), :], by, 1) for block, by in found]
                way, at = divmod(slab, BS // 2)
                keep[h, way, q, pl.ds(at, SLAB), :] = regroup(group, parts)
            return carry

        lax.fori_loop(0, PACKS, one, 0)

    def pass_on(h):
        for way in range(2):
            hop_copy(h, way).wait_recv()
            last_copy(h, way).start()

    def step(g, carry):
        h = lax.div(g, STEPS)
        s = lax.rem(g, STEPS)
        for role in (0, 1):
            for at, (name, turn_index) in enumerate(WAITS[role]):
                @pl.when(is_role[role] & (s == at))
                def _():
                    unit_copy(link_of(name), name, h, turn_index, turn_index).wait_recv()
                    sent_on = RELAYS[role].get(name)
                    if sent_on is not None:
                        unit_copy(link_of(sent_on[0]), sent_on[0], h, sent_on[1], sent_on[2]).start()
                    if role == 0 and name == "zE0":
                        @pl.when(h == 0)
                        def _():
                            mark_copy(0, 2, inner, 0).wait_recv()
                            mark_copy(2, 1, inner, 1).start()
                    if role == 1 and name == "yE0":
                        @pl.when(h == 0)
                        def _():
                            mark_copy(0, 1, inner, 0).wait_recv()
                            mark_copy(1, 3, down, 2).start()
                    if role == 1 and name == "zB":
                        @pl.when(h == 0)
                        def _():
                            mark_copy(0, 2, inner, 0).wait_recv()
                            mark_copy(2, 3, inner, 3).start()

                    @pl.when(h < STRIPS - 1)
                    def _():
                        for own_name, target, after in OWN[role]:
                            if after == at:
                                unit_copy(link_of(own_name), own_name, h + 1, 0, target).start()

        @pl.when(g == by_role(odd, LEFT_RELAY[0], LEFT_RELAY[1]))
        def _():
            x_copy(2, 0, left, 0).wait_recv()

            @pl.when(core == 0)
            def _():
                x_copy(1, 2, sibling, 2).start()

            @pl.when(core == 1)
            def _():
                x_copy(3, 2, sibling, 2).start()

        @pl.when(g == by_role(odd, LEFT_READY[0], LEFT_READY[1]))
        def _():
            x_copy(1, 0, sibling, 1).wait_recv()
            x_copy(3, 0, sibling, 1).wait_recv()
            for role in (0, 1):
                @pl.when(is_role[role])
                def _():
                    for turn_index in ((1, 3), (3,))[role]:
                        mark_copy(0, turn_index, inner, 0).wait_recv()

            def one(i, c):
                fill_left(i)
                fill_wheres(i)
                return c

            lax.fori_loop(1, 4, one, 0)

        for strip in range(STRIPS - 1):
            @pl.when(g == by_role(odd, PASS_ON[0][strip], PASS_ON[1][strip]))
            def _():
                pass_on(strip)

        before = by_role(odd, lookup(g, [0] + DONE[0]), lookup(g, [0] + DONE[1]))
        after = by_role(odd, lookup(g, DONE[0]), lookup(g, DONE[1]))

        def task(i, c):
            q = before + i

            @pl.when(q < after)
            def _():
                j = lax.rem(q, TASKS)
                code = by_role(odd, lookup(j, ORDER[0]), lookup(j, ORDER[1]))
                products(lax.div(q, TASKS), lax.div(code, HALVES), lax.rem(code, HALVES))

            return c

        lax.fori_loop(0, MOST, task, 0)

        @pl.when(lax.div(after, TASKS) > lax.div(before, TASKS))
        def _():
            strip = lax.div(before, TASKS)
            gather(strip, OWNED * (1 - rep), stage)
            for way in range(2):
                hop_copy(strip, way).start()
            gather(strip, OWNED * rep, own)

        return carry

    lax.fori_loop(0, STRIPS * STEPS, step, 0)
    pass_on(STRIPS - 1)

    def finish_wait(h, carry):
        for way in range(2):
            last_copy(h, way).wait_recv()
        return carry

    lax.fori_loop(0, STRIPS, finish_wait, 0)

    def finish(i, carry):
        q = lax.div(i, 2)
        way = lax.rem(i, 2)
        for slab in range(0, BS // 2, SLAB):
            part = pl.ds(slab, SLAB)
            whole = [own[h, way, q, part, :] + arrived[h, way, q, part, :] for h in range(STRIPS)]
            at = pl.ds(pl.multiple_of(way * (BS // 2) + slab, SLAB), SLAB)
            for b in range(STRIPS):
                out[q * STRIPS + b, at, :] = regroup(group, [shifted(whole[h], h - b) for h in range(STRIPS)])
        return carry

    lax.fori_loop(0, 2 * PACKS, finish, 0)

    def sent(h, carry):
        for role in (0, 1):
            @pl.when(is_role[role])
            def _():
                names = [name for name, _, _ in RELAYS[role].values()] + [name for name, _, _ in OWN[role]]
                for name in names:
                    unit_copy(link_of(name), name, h, 0, 0).wait_send()

        for way in range(2):
            hop_copy(h, way).wait_send()
            last_copy(h, way).wait_send()
        return carry

    lax.fori_loop(0, STRIPS, sent, 0)
    for role in (0, 1):
        @pl.when(is_role[role])
        def _():
            for lane in range((2, 4)[role]):
                mark_copy(0, 1, inner, lane).wait_send()
    for lane in range(3):
        x_copy(1, 0, left, lane).wait_send()


def shards(rows, columns, left_values, left_rows, right_values, right_cols, result_slots):
    left = left_values.reshape(2, KB * LPB * BS, BS)
    right = right_values.reshape(KB * BPR, BS, BS)
    vmem = pltpu.VMEM
    dma = pltpu.SemaphoreType.DMA
    out = pl.pallas_call(
        functools.partial(kernel, rows, columns),
        out_shape=jax.ShapeDtypeStruct((OWNED, BS, BS), f32),
        in_specs=[pl.BlockSpec(memory_space=pltpu.HBM)] * 5,
        out_specs=pl.BlockSpec(memory_space=vmem),
        scratch_shapes=[
            vmem((KB * BPR, BS, BS), f32),
            vmem((STRIPS, 4, KB * BS, BS), f32),
            vmem((5, KB * LPB * BS + 16, BS), f32),
            vmem((4, 2, 2, RB * BS, HALF * BS), bf16),
            vmem((2, HALF * BS // 2, 2 * BS), bf16),
            vmem((2, HALF * BS // 2, 2 * BS), bf16),
            vmem((STRIPS * CB, BS, BS), f32),
            vmem((STRIPS, 2, PACKS, BS // 2, BS), f32),
            vmem((STRIPS, 2, PACKS, BS // 2, BS), f32),
            vmem((STRIPS, 2, PACKS, BS // 2, BS), f32),
            vmem((STRIPS, 2, PACKS, BS // 2, BS), f32),
            vmem((4, 8, BS), f32),
            vmem((4, KB, STRIPS, 8, BS), f32),
            pltpu.SMEM((2, LPB, KB), jnp.int32),
            pltpu.SMEM((BPR, KB), jnp.int32),
            pltpu.SMEM((1, NC), jnp.int32),
            dma((2,)), dma((2,)), dma((3,)),
            dma((STRIPS, 6)), dma((STRIPS, 6)), dma((STRIPS, 5)), dma((STRIPS, 5)),
            dma((3,)), dma((3,)), dma((4,)), dma((3,)),
            dma((STRIPS, 2)), dma((STRIPS, 2)), dma((STRIPS, 2)), dma((STRIPS, 2)),
        ],
        compiler_params=pltpu.CompilerParams(
            collective_id=0, has_side_effects=True, vmem_limit_bytes=VMEM_LIMIT
        ),
    )(
        left, right, left_rows.reshape(2, KB, LPB).transpose(0, 2, 1), right_cols.reshape(KB, BPR).T,
        result_slots.reshape(1, NC),
    )
    return out[None, None]


def solution(mesh):
    in_specs = (
        P("row", "rep", "col", None, None, None, None, None),
        P("row", "rep", "col", None, None, None),
        P("rep", "row", "col", None, None, None, None),
        P("rep", "row", "col", None, None),
        P("row", "col", None),
    )
    out_specs = P("row", "col", "rep", None, None)
    body = functools.partial(shards, mesh.shape["row"], mesh.shape["col"])
    return jax.shard_map(body, mesh=mesh, in_specs=in_specs, out_specs=out_specs, check_vma=False)
```

```python
import functools

import jax
import jax.numpy as jnp
from jax import lax
from jax.experimental import pallas as pl
from jax.experimental.pallas import tpu as pltpu
from jax.sharding import PartitionSpec as P

BS = 128
KB = 8
BPR = 4
LPB = 2
RB = 4
CB = 8
NC = 24
STRIPS = 4
LANES = BS // STRIPS
OWNED = NC // 2
PACKS = OWNED // STRIPS
HALVES = 2
HALF = KB // HALVES
TASKS = 4 * HALVES
SLAB = 32
VMEM_LIMIT = 60 * 2**20
MESH = pl.DeviceIdType.MESH
f32 = jnp.float32
bf16 = jnp.bfloat16

IN_A = 2
IN_B = 4
SLOT = {
    "zE0": (0, 0, 2), "zE1": (1, 2, 2), "zE2": (2, 4, 2), "zE3": (3, 6, 2), "zA": (4, 0, IN_A), "zB": (4, IN_A, IN_B),
    "zD": (5, IN_A + IN_B, KB - IN_A - IN_B),
    "yE0": (0, 0, 2), "yE1": (1, 2, 2), "yE2": (2, 4, 2), "yE3": (3, 6, 2), "yA": (4, 0, IN_A),
    "oA": (0, 0, IN_A), "oB": (1, IN_A, IN_B), "oD": (2, IN_A + IN_B, KB - IN_A - IN_B), "ob": (3, IN_A, IN_B),
}
WAITS = {
    0: [('zE0', 2), ('zE1', 2), ('oA', 1), ('zE2', 2), ('zE3', 2), ('oD', 1), ('zA', 3), ('zD', 3), ('oB', 1), ('ob', 3)],
    1: [('yE0', 1), ('zB', 2), ('yE1', 1), ('yE2', 1), ('zD', 2), ('yE3', 1), ('zE0', 3), ('zE1', 3), ('yA', 2), ('zE3', 3), ('zE2', 3)],
}
RELAYS = {
    0: {"zE0": ("yE0", 2, 1), "zE1": ("yE1", 2, 1), "zE2": ("yE2", 2, 1), "zE3": ("yE3", 2, 1),
        "zA": ("yA", 3, 2), "oA": ("zA", 1, 3), "oD": ("zD", 1, 3)},
    1: {"zB": ("ob", 2, 3), "yE0": ("zE0", 1, 3), "yE1": ("zE1", 1, 3), "yE2": ("zE2", 1, 3), "yE3": ("zE3", 1, 3)},
}
OWN = {
    0: [('zE0', 2, 5), ('zE1', 2, 6), ('zE2', 2, 6), ('zE3', 2, 8)],
    1: [('zB', 2, 5), ('oA', 1, 5), ('oB', 1, 6), ('oD', 1, 6), ('zD', 2, 10)],
}
STEPS = 11
PASS_ON = {0: [38, 39, 42], 1: [25, 38, 40]}
LEFT_RELAY = {0: 14, 1: 14}
LEFT_READY = {0: 17, 1: 17}
DONE = {
    0: [2, 2, 2, 2, 2, 2, 2, 2, 2, 2, 2, 2, 2, 2, 2, 2, 2, 3, 4, 5, 6, 6, 7, 8, 9, 10, 11, 12, 13, 14, 15, 16, 16, 18, 20, 22, 24, 26, 28, 28, 28, 30, 32, 32],
    1: [1, 2, 2, 2, 2, 2, 2, 2, 2, 2, 2, 2, 2, 2, 2, 2, 2, 4, 6, 8, 10, 12, 13, 14, 15, 16, 17, 18, 19, 20, 21, 22, 23, 24, 25, 26, 27, 28, 29, 29, 30, 31, 31, 32],
}
ORDER = {
    0: [0, 1, 4, 5, 2, 3, 6, 7],
    1: [0, 1, 2, 5, 3, 6, 4, 7],
}
MOST = max(b - a for role in (0, 1) for a, b in zip([0] + DONE[role], DONE[role]))


def by_role(odd, even_value, odd_value):
    return even_value + odd * (odd_value - even_value)


def lookup(index, values):
    found = jnp.int32(values[0])
    for at in range(1, len(values)):
        if values[at] != values[at - 1]:
            found = found + jnp.where(index >= at, values[at] - values[at - 1], 0)
    return found


def regroup(group, parts):
    picked = parts[STRIPS - 1]
    for b in range(STRIPS - 2, -1, -1):
        picked = jnp.where(group == b, parts[b], picked)
    return picked


def shifted(x, groups):
    by = (groups * LANES) % BS
    return x if by == 0 else pltpu.roll(x, by, 1)


def kernel(
    rows, columns,
    left_hbm, right_hbm, left_rows_hbm, right_cols_hbm, slots_hbm, out,
    raw, units, panels, left_parts, right_first, right_second, sums,
    own, stage, relay, arrived, marks, wheres, left_rows, right_cols, slots,
    load_sem, left_load_sem, small_sem, z_send, z_recv, y_send, y_recv, x_send, x_recv,
    mark_send, mark_recv, hop_send, hop_recv, last_send, last_recv,
):
    row = lax.axis_index("row")
    col = lax.axis_index("col")
    rep = lax.axis_index("rep")
    odd = lax.rem(row, 2)
    core = lax.rem(col, 2)
    chip = lax.div(col, 2)
    is_role = {0: odd == 0, 1: odd == 1}
    mate_row = row + 1 - 2 * odd
    up = (lax.rem(row + 2, rows), col, rep)
    down = (lax.rem(row + rows - 2, rows), col, rep)
    inner = (mate_row, col, rep)
    outer = (mate_row, col, 1 - rep)
    sibling = (row, col + 1 - 2 * core, rep)
    right = (row, lax.rem(col + 2, columns), rep)
    left = (row, lax.rem(col + columns - 2, columns), rep)
    far = (row, lax.rem(col - core + 4, columns) + 1 - core, rep)

    barrier = pltpu.get_barrier_semaphore()
    peers = (up, down, inner, outer, sibling, right, left, far)
    for peer in peers:
        pl.semaphore_signal(barrier, inc=1, device_id=peer, device_id_type=MESH)

    small = [
        pltpu.make_async_copy(right_cols_hbm, right_cols, small_sem.at[0]),
        pltpu.make_async_copy(left_rows_hbm, left_rows, small_sem.at[1]),
        pltpu.make_async_copy(slots_hbm, slots, small_sem.at[2]),
    ]

    def load_right(half):
        part = pl.ds(half * KB * BPR // 2, KB * BPR // 2)
        return pltpu.make_async_copy(right_hbm.at[part], raw.at[part], load_sem.at[half])

    def load_left(slot):
        return pltpu.make_async_copy(
            left_hbm.at[slot], panels.at[4 * slot, pl.ds(0, KB * LPB * BS)], left_load_sem.at[slot]
        )

    small[0].start()
    for half in range(2):
        load_right(half).start()
    small[1].start()
    small[2].start()
    for slot in range(2):
        load_left(slot).start()

    group = lax.broadcasted_iota(jnp.int32, (SLAB, BS), 1) // LANES
    sub8 = lax.broadcasted_iota(jnp.int32, (8, BS), 0)
    group8 = lax.broadcasted_iota(jnp.int32, (8, BS), 1) // LANES

    def pack(h, k):
        for slab in range(0, BS, SLAB):
            parts = [
                pltpu.roll(
                    raw[k * BPR + b, pl.ds(slab, SLAB), :], lax.rem(jnp.int32(b + STRIPS) - h, STRIPS) * LANES, 1
                )
                for b in range(BPR)
            ]
            units[h, 0, pl.ds(pl.multiple_of(k * BS + slab, SLAB), SLAB), :] = regroup(group, parts)

    def unit_copy(link, name, h, source, target):
        slot, first, count = SLOT[name]
        sends, recvs, peer = (z_send, z_recv, down) if link == "z" else (y_send, y_recv, inner)
        return pltpu.make_async_remote_copy(
            src_ref=units.at[h, source, pl.ds(first * BS, count * BS)],
            dst_ref=units.at[h, target, pl.ds(first * BS, count * BS)],
            send_sem=sends.at[h, slot], recv_sem=recvs.at[h, slot], device_id=peer, device_id_type=MESH,
        )

    def link_of(name):
        return "z" if name[0] == "z" else "y"

    def x_copy(turn_index, source, peer, lane):
        return pltpu.make_async_remote_copy(
            src_ref=panels.at[source], dst_ref=panels.at[turn_index],
            send_sem=x_send.at[lane], recv_sem=x_recv.at[turn_index - 1],
            device_id=peer, device_id_type=MESH,
        )

    def mark_copy(source, target, peer, lane):
        return pltpu.make_async_remote_copy(
            src_ref=marks.at[source], dst_ref=marks.at[target],
            send_sem=mark_send.at[lane], recv_sem=mark_recv.at[target - 1],
            device_id=peer, device_id_type=MESH,
        )

    def hop_copy(h, way):
        return pltpu.make_async_remote_copy(
            src_ref=stage.at[h, way], dst_ref=relay.at[h, way],
            send_sem=hop_send.at[h, way], recv_sem=hop_recv.at[h, way],
            device_id=(inner, outer)[way], device_id_type=MESH,
        )

    def last_copy(h, way):
        return pltpu.make_async_remote_copy(
            src_ref=relay.at[h, way], dst_ref=arrived.at[h, way],
            send_sem=last_send.at[h, way], recv_sem=last_recv.at[h, way],
            device_id=(outer, inner)[way], device_id_type=MESH,
        )

    small[0].wait()
    places = jnp.zeros((8, BS), f32)
    for b in range(BPR):
        for k in range(KB):
            places = jnp.where((group8 == b) & (sub8 == k), right_cols[b, k].astype(f32), places)
    marks[0] = places

    def pack_first(k, carry):
        pack(0, k)
        return carry

    for half in range(2):
        load_right(half).wait()
        lax.fori_loop(half * KB // 2, (half + 1) * KB // 2, pack_first, 0)
    pl.semaphore_wait(barrier, len(peers))

    for role in (0, 1):
        @pl.when(is_role[role])
        def _():
            if role == 0:
                mark_copy(0, 2, down, 0).start()
            else:
                mark_copy(0, 1, inner, 0).start()
                mark_copy(0, 2, down, 1).start()
            for name, target, _ in OWN[role]:
                unit_copy(link_of(name), name, 0, 0, target).start()

    small[1].wait()
    for slot in range(2):
        load_left(slot).wait()
        for a in range(LPB):
            places = jnp.zeros((8, BS), f32)
            for k in range(KB):
                places = jnp.where(sub8 == k, left_rows[slot, a, k].astype(f32), places)
            panels[4 * slot, pl.ds(KB * LPB * BS + 8 * a, 8), :] = places

    x_copy(2, jnp.where(chip == 0, 4, 0), left, 0).start()

    @pl.when(core == 0)
    def _():
        x_copy(3, jnp.where(chip < 2, 4, 0), far, 1).start()

    @pl.when(core == 1)
    def _():
        x_copy(1, 0, sibling, 1).start()

    small[2].wait()

    def row_of(tile, k):
        one = jnp.sum(jnp.where(sub8 == k, tile, 0.0), axis=0, keepdims=True)
        return jnp.broadcast_to(one, (8, BS))

    def tall(x):
        return x.reshape(SLAB // 8, 8, BS)

    def fill_left(turn_index):
        def one(k, carry):
            half = lax.div(k, HALF)
            at = pl.ds(pl.multiple_of(lax.rem(k, HALF) * BS, BS), BS)
            where = [row_of(panels[turn_index, pl.ds(KB * LPB * BS + 8 * a, 8), :], k) for a in range(LPB)]
            for slab in range(0, BS, SLAB):
                blocks = [
                    tall(panels[turn_index, pl.ds(pl.multiple_of((k * LPB + a) * BS + slab, SLAB), SLAB), :])
                    for a in range(LPB)
                ]
                for r in range(RB):
                    second = jnp.where((where[1] == r)[None], blocks[1], 0.0)
                    block = jnp.where((where[0] == r)[None], blocks[0], second).reshape(SLAB, BS)
                    hi = block.astype(bf16)
                    lo = (block - hi.astype(f32)).astype(bf16)
                    for part, value in enumerate((hi, lo)):
                        left_parts[turn_index, half, part, pl.ds(r * BS + slab, SLAB), at] = value
            return carry

        lax.fori_loop(0, KB, one, 0)

    def fill_wheres(turn_index):
        tile = marks[turn_index]
        for k in range(KB):
            mine = row_of(tile, k)
            for turned in range(STRIPS):
                wheres[turn_index, k, turned] = shifted(mine, STRIPS - turned)


    def products(h, turn_index, half):
        got = None
        depth = HALF * BS // 2
        for pair, right_parts in enumerate((right_first, right_second)):
            for kk in range(2):
                k = half * HALF + pair * 2 + kk
                places = [wheres[turn_index, k, turned] for turned in range(STRIPS)]
                masks = [[(place == (group8 + 4 * u).astype(f32))[None] for place in places] for u in range(2)]
                for slab in range(0, BS, SLAB):
                    packed = units[h, turn_index, pl.ds(pl.multiple_of(k * BS + slab, SLAB), SLAB), :]
                    blocks = [tall(shifted(packed, STRIPS - turned)) for turned in range(STRIPS)]
                    at = pl.ds(kk * BS + slab, SLAB)
                    for u in range(2):
                        terms = [jnp.where(mask, block, 0.0) for mask, block in zip(masks[u], blocks)]
                        whole = ((terms[0] + terms[1]) + (terms[2] + terms[3])).reshape(SLAB, BS)
                        hi = whole.astype(bf16)
                        right_parts[0, at, u * BS:(u + 1) * BS] = hi
                        right_parts[1, at, u * BS:(u + 1) * BS] = (whole - hi.astype(f32)).astype(bf16)
        for pair, right_parts in enumerate((right_first, right_second)):
            for left_part, right_part in ((0, 0), (1, 0), (0, 1)):
                mine = left_parts[turn_index, half, left_part, :, pair * depth:(pair + 1) * depth]
                term = jnp.dot(mine, right_parts[right_part], preferred_element_type=f32)
                got = term if got is None else got + term
        for u in range(2):
            for r in range(RB):
                sums[h * CB + u * RB + r] += got[r * BS:(r + 1) * BS, u * BS:(u + 1) * BS]

    def gather(h, first, keep):
        def one(q, carry):
            found = []
            for b in range(STRIPS):
                slot = slots[0, first + q * STRIPS + b]
                c = lax.rem(slot, CB)
                away = lax.rem(b - lax.rem(c, 4) + STRIPS, STRIPS)
                found.append((h * CB + lax.div(c, 4) * RB + lax.div(slot, CB), away * LANES))
            for slab in range(0, BS, SLAB):
                parts = [pltpu.roll(sums[block, pl.ds(slab, SLAB), :], by, 1) for block, by in found]
                way, at = divmod(slab, BS // 2)
                keep[h, way, q, pl.ds(at, SLAB), :] = regroup(group, parts)
            return carry

        lax.fori_loop(0, PACKS, one, 0)

    def pass_on(h):
        for way in range(2):
            hop_copy(h, way).wait_recv()
            last_copy(h, way).start()

    def step(g, carry):
        h = lax.div(g, STEPS)
        s = lax.rem(g, STEPS)
        for role in (0, 1):
            for at, (name, turn_index) in enumerate(WAITS[role]):
                @pl.when(is_role[role] & (s == at))
                def _():
                    unit_copy(link_of(name), name, h, turn_index, turn_index).wait_recv()
                    sent_on = RELAYS[role].get(name)
                    if sent_on is not None:
                        unit_copy(link_of(sent_on[0]), sent_on[0], h, sent_on[1], sent_on[2]).start()
                    if role == 0 and name == "zE0":
                        @pl.when(h == 0)
                        def _():
                            mark_copy(0, 2, inner, 0).wait_recv()
                            mark_copy(2, 1, inner, 1).start()
                    if role == 1 and name == "yE0":
                        @pl.when(h == 0)
                        def _():
                            mark_copy(0, 1, inner, 0).wait_recv()
                            mark_copy(1, 3, down, 2).start()
                    if role == 1 and name == "zB":
                        @pl.when(h == 0)
                        def _():
                            mark_copy(0, 2, inner, 0).wait_recv()
                            mark_copy(2, 3, inner, 3).start()

                    @pl.when(h < STRIPS - 1)
                    def _():
                        for own_name, target, after in OWN[role]:
                            if after == at:
                                unit_copy(link_of(own_name), own_name, h + 1, 0, target).start()

        @pl.when(g == 0)
        def _():
            fill_left(0)
            fill_wheres(0)
            sums[...] = jnp.zeros_like(sums)

        @pl.when((s == 1) & (h < STRIPS - 1))
        def _():
            def pack_next(k, c):
                pack(h + 1, k)
                return c

            lax.fori_loop(0, KB, pack_next, 0)

        @pl.when(g == by_role(odd, LEFT_RELAY[0], LEFT_RELAY[1]))
        def _():
            x_copy(2, 0, left, 0).wait_recv()

            @pl.when(core == 0)
            def _():
                x_copy(1, 2, sibling, 2).start()

            @pl.when(core == 1)
            def _():
                x_copy(3, 2, sibling, 2).start()

            fill_left(2)
            fill_wheres(2)

        @pl.when(g == by_role(odd, LEFT_READY[0], LEFT_READY[1]))
        def _():
            x_copy(1, 0, sibling, 1).wait_recv()
            x_copy(3, 0, sibling, 1).wait_recv()
            for role in (0, 1):
                @pl.when(is_role[role])
                def _():
                    for turn_index in ((1, 3), (3,))[role]:
                        mark_copy(0, turn_index, inner, 0).wait_recv()

            def one(i, c):
                fill_left(1 + 2 * i)
                fill_wheres(1 + 2 * i)
                return c

            lax.fori_loop(0, 2, one, 0)

        for strip in range(STRIPS - 1):
            @pl.when(g == by_role(odd, PASS_ON[0][strip], PASS_ON[1][strip]))
            def _():
                pass_on(strip)

        before = by_role(odd, lookup(g, [0] + DONE[0]), lookup(g, [0] + DONE[1]))
        after = by_role(odd, lookup(g, DONE[0]), lookup(g, DONE[1]))

        def task(i, c):
            q = before + i

            @pl.when(q < after)
            def _():
                j = lax.rem(q, TASKS)
                code = by_role(odd, lookup(j, ORDER[0]), lookup(j, ORDER[1]))
                products(lax.div(q, TASKS), lax.div(code, HALVES), lax.rem(code, HALVES))

            return c

        lax.fori_loop(0, MOST, task, 0)

        @pl.when(lax.div(after, TASKS) > lax.div(before, TASKS))
        def _():
            strip = lax.div(before, TASKS)
            gather(strip, OWNED * (1 - rep), stage)
            for way in range(2):
                hop_copy(strip, way).start()
            gather(strip, OWNED * rep, own)

        return carry

    lax.fori_loop(0, STRIPS * STEPS, step, 0)
    pass_on(STRIPS - 1)

    def finish_wait(h, carry):
        for way in range(2):
            last_copy(h, way).wait_recv()
        return carry

    lax.fori_loop(0, STRIPS, finish_wait, 0)

    def finish(i, carry):
        q = lax.div(i, 2)
        way = lax.rem(i, 2)
        for slab in range(0, BS // 2, SLAB):
            part = pl.ds(slab, SLAB)
            whole = [own[h, way, q, part, :] + arrived[h, way, q, part, :] for h in range(STRIPS)]
            at = pl.ds(pl.multiple_of(way * (BS // 2) + slab, SLAB), SLAB)
            for b in range(STRIPS):
                out[q * STRIPS + b, at, :] = regroup(group, [shifted(whole[h], h - b) for h in range(STRIPS)])
        return carry

    lax.fori_loop(0, 2 * PACKS, finish, 0)

    def sent(h, carry):
        for role in (0, 1):
            @pl.when(is_role[role])
            def _():
                names = [name for name, _, _ in RELAYS[role].values()] + [name for name, _, _ in OWN[role]]
                for name in names:
                    unit_copy(link_of(name), name, h, 0, 0).wait_send()

        for way in range(2):
            hop_copy(h, way).wait_send()
            last_copy(h, way).wait_send()
        return carry

    lax.fori_loop(0, STRIPS, sent, 0)
    for role in (0, 1):
        @pl.when(is_role[role])
        def _():
            for lane in range((2, 4)[role]):
                mark_copy(0, 1, inner, lane).wait_send()
    for lane in range(3):
        x_copy(1, 0, left, lane).wait_send()


def shards(rows, columns, left_values, left_rows, right_values, right_cols, result_slots):
    left = left_values.reshape(2, KB * LPB * BS, BS)
    right = right_values.reshape(KB * BPR, BS, BS)
    vmem = pltpu.VMEM
    dma = pltpu.SemaphoreType.DMA
    out = pl.pallas_call(
        functools.partial(kernel, rows, columns),
        out_shape=jax.ShapeDtypeStruct((OWNED, BS, BS), f32),
        in_specs=[pl.BlockSpec(memory_space=pltpu.HBM)] * 5,
        out_specs=pl.BlockSpec(memory_space=vmem),
        scratch_shapes=[
            vmem((KB * BPR, BS, BS), f32),
            vmem((STRIPS, 4, KB * BS, BS), f32),
            vmem((5, KB * LPB * BS + 16, BS), f32),
            vmem((4, 2, 2, RB * BS, HALF * BS), bf16),
            vmem((2, HALF * BS // 2, 2 * BS), bf16),
            vmem((2, HALF * BS // 2, 2 * BS), bf16),
            vmem((STRIPS * CB, BS, BS), f32),
            vmem((STRIPS, 2, PACKS, BS // 2, BS), f32),
            vmem((STRIPS, 2, PACKS, BS // 2, BS), f32),
            vmem((STRIPS, 2, PACKS, BS // 2, BS), f32),
            vmem((STRIPS, 2, PACKS, BS // 2, BS), f32),
            vmem((4, 8, BS), f32),
            vmem((4, KB, STRIPS, 8, BS), f32),
            pltpu.SMEM((2, LPB, KB), jnp.int32),
            pltpu.SMEM((BPR, KB), jnp.int32),
            pltpu.SMEM((1, NC), jnp.int32),
            dma((2,)), dma((2,)), dma((3,)),
            dma((STRIPS, 6)), dma((STRIPS, 6)), dma((STRIPS, 5)), dma((STRIPS, 5)),
            dma((3,)), dma((3,)), dma((4,)), dma((3,)),
            dma((STRIPS, 2)), dma((STRIPS, 2)), dma((STRIPS, 2)), dma((STRIPS, 2)),
        ],
        compiler_params=pltpu.CompilerParams(
            collective_id=0, has_side_effects=True, vmem_limit_bytes=VMEM_LIMIT
        ),
    )(
        left, right, left_rows.reshape(2, KB, LPB).transpose(0, 2, 1), right_cols.reshape(KB, BPR).T,
        result_slots.reshape(1, NC),
    )
    return out[None, None]


def solution(mesh):
    in_specs = (
        P("row", "rep", "col", None, None, None, None, None),
        P("row", "rep", "col", None, None, None),
        P("rep", "row", "col", None, None, None, None),
        P("rep", "row", "col", None, None),
        P("row", "col", None),
    )
    out_specs = P("row", "col", "rep", None, None)
    body = functools.partial(shards, mesh.shape["row"], mesh.shape["col"])
    return jax.shard_map(body, mesh=mesh, in_specs=in_specs, out_specs=out_specs, check_vma=False)
```
